32 devices in a mesh: dp: 8 (over y, x, core), mp: 4 (over z).
Axes of the slice: x: 2, y: 2, z: 4, core: 2. Of those that a mesh axis runs over, the one named last changes fastest.
Arguments:
- tokens: bfloat16 [16384, 1024], P('dp'), may hold values from -6 to 6
- cotangent: bfloat16 [16384, 1024], P('dp'), may hold values from -6 to 6
- lengths: int32 [8, 12], P('dp'), may hold values from 1 to 1024, 2048 in all within a row
- norm_params: float32 [4, 1024], replicated, as said below
- joined_weight: bfloat16 [1024, 3072], P(None, 'mp'), may hold values from -0.1875 to 0.1875
- b_qkv: bfloat16 [3072], P('mp'), may hold values from -1.25 to 1.25
- output_weight: bfloat16 [1024, 1024], P('mp'), may hold values from -1 to 1
- b_o: bfloat16 [1024], replicated, may hold values from -1.25 to 1.25
- up_weight: bfloat16 [1024, 4096], P(None, 'mp'), may hold values from -0.1875 to 0.1875
- b_up: bfloat16 [4096], P('mp'), may hold values from -1.25 to 1.25
- down_weight: bfloat16 [4096, 1024], P('mp'), may hold values from -0.09375 to 0.09375
- b_down: bfloat16 [1024], replicated, may hold values from -1.25 to 1.25
- shared_factors: float32 [4, 1024, 128], P(None, ('dp', 'mp')), as said below
- shared_moments: float32 [2, 4, 1024, 128], P(None, None, ('dp', 'mp')), as said below
- local_factors: float32 [4, 3072, 128], P('mp', 'dp'), as said below
- local_moments: float32 [2, 4, 3072, 128], P(None, 'mp', 'dp'), as said below
Outputs:
- out: bfloat16 [16384, 1024], P('dp')
- input_grad: bfloat16 [16384, 1024], P('dp')
- norm_grads: float32 [4, 1024], P(None, ('dp', 'mp'))
- shared_grads: float32 [4, 1024, 128], P(None, ('dp', 'mp'))
- local_grads: float32 [4, 3072, 128], P('mp', 'dp')
- joined_weight_merged: bfloat16 [1024, 3072], P(None, 'mp')
- output_weight_merged: bfloat16 [1024, 1024], P('mp')
- up_weight_merged: bfloat16 [1024, 4096], P(None, 'mp')
- down_weight_merged: bfloat16 [4096, 1024], P('mp')
- stepped_shared_factors: float32 [4, 1024, 128], P(None, ('dp', 'mp'))
- new_local: float32 [4, 3072, 128], P('mp', 'dp')
- shared_state: float32 [2, 4, 1024, 128], P(None, None, ('dp', 'mp'))
- local_state: float32 [2, 4, 3072, 128], P(None, 'mp', 'dp')
The draws below stay inside these ranges and needn't reach their ends.
Inputs may be any that keep to these rules, and one draw needn't show every extreme that they name: Each row's 12 lengths sum to 2048; the largest of each row is exactly 1024. `norm_params`: rows 0 and 2 are gains between 0.7 and 1.3. `shared_factors`: entries of order 1024^-0.5 for the a factors and 128^-0.5 for the b factors. `local_factors`: entries of order 128^-0.5 for b factors, 32^-0.5 for a_o and 4096^-0.5 for a_down. `shared_moments`: the second moments (index 1 of the first dimension) are positive. `local_moments`: the second moments (index 1 of the first dimension) are positive.
All inputs are finite; a program needn't handle non-finite values.
Results may differ from the reference program's by a relative error of at most 0.005.
The reference program's roundings to bfloat16 on the way count: a program that leaves them out, or rounds other values in their place, can miss the bound.
Values may be sent and summed in bfloat16 or wider, within the bound.
No kernel may reach another device: no remote copies, remote signals or barrier semaphores. Data moves between devices by JAX's collectives and lax.ppermute only.
A program may use at most 192 MiB of HBM per device.

```python
import math
import jax
import jax.numpy as jnp
import numpy as np
from jax import lax

D = 1024
FF = 4096
HEADS = 16
HD = 64
ADAPTER_RANK = 128
ROT = 16
TOK_DEV = 2048
QB = 512
SLOTS = 12
LONGEST = 1024
TOKENS = 16384
LROWS = 3072
N_DP = 8
N_MP = 4


def draw_norm_params(key, part):
    base = jax.random.fold_in(key, 101)
    gains = jax.random.uniform(jax.random.fold_in(base, 1), (4, D), jnp.float32, 0.7, 1.3)
    shifts = 0.2 * jax.random.normal(jax.random.fold_in(base, 2), (4, D), jnp.float32)
    which = lax.broadcasted_iota(jnp.int32, (4, D), 0)
    return jnp.where(which % 2 == 0, gains, shifts)


def draw_shared_factors(key, part):
    base = jax.random.fold_in(key, 202)
    raw = jax.random.truncated_normal(base, -3.0, 3.0, (4, D, ADAPTER_RANK), jnp.float32)
    which = lax.broadcasted_iota(jnp.int32, (4, D, ADAPTER_RANK), 0)
    factor_scale = jnp.where(which < 2, D ** (-0.5), ADAPTER_RANK ** (-0.5))
    return raw * factor_scale


def draw_local_factors(key, part):
    base = jax.random.fold_in(key, 303)
    raw = jax.random.truncated_normal(base, -3.0, 3.0, (N_MP, LROWS, ADAPTER_RANK), jnp.float32)
    which = lax.broadcasted_iota(jnp.int32, (N_MP, LROWS, ADAPTER_RANK), 1)
    first_end = 3 * D // N_MP + FF // N_MP
    second_end = first_end + D // N_MP
    factor_scale = jnp.where(which < first_end, ADAPTER_RANK ** (-0.5), jnp.where(which < second_end, (D // 32) ** (-0.5), FF ** (-0.5)))
    return raw * factor_scale


def moment_pair(key, shape):
    first = 2.0 * jax.random.normal(jax.random.fold_in(key, 1), shape, jnp.float32)
    second = jnp.exp(jax.random.uniform(jax.random.fold_in(key, 2), shape, jnp.float32, math.log(0.001), math.log(0.1)))
    return jnp.stack([first, second])


def draw_shared_moments(key, part):
    return moment_pair(jax.random.fold_in(key, 404), (4, D, ADAPTER_RANK))


def draw_local_moments(key, part):
    return moment_pair(jax.random.fold_in(key, 505), (N_MP, LROWS, ADAPTER_RANK))


def steps_of(stream_key, shape, shards, least, high):
    loudness = 1.0
    for dim, parts in shards:
        draws = jax.random.uniform(jax.random.fold_in(jax.random.fold_in(stream_key, 6), dim), (parts,), jnp.float32, least / len(shards), high / len(shards))
        loudness = loudness * jnp.repeat(jnp.exp(draws), shape[dim] // parts).reshape((-1,) + (1,) * (len(shape) - 1 - dim))
    return loudness


def split_up(number_of, total, most, slope):
    portions = [(1 << 20) // math.isqrt(standing ** slope) + 1 for standing in range(2, number_of + 1)]
    surplus, given = total - most - (number_of - 1), [1] * (number_of - 1)
    while surplus > 0:
        movable = [i for i in range(number_of - 1) if given[i] < most]
        whole, budget = sum([portions[i] for i in movable]), surplus
        for i in movable:
            addition = min(most - given[i], max(1, budget * portions[i] // whole), surplus)
            given[i] = given[i] + addition
            surplus = surplus - addition
    return np.array([most] + given)


def uneven_parts(stream_key, number_of, total, bound, slope):
    if number_of == 2:
        one = jax.random.randint(stream_key, (), max(1, total - bound), min(bound, total - 1) + 1)
        return jnp.stack([one, total - one])
    sizes = jnp.asarray(split_up(number_of, total, bound, slope), jnp.int32)
    pairs = (number_of - 1) // 2
    donor, taker = sizes[1:1 + 2 * pairs:2], sizes[2:2 + 2 * pairs:2]
    slack = jnp.minimum(donor - 1, bound - taker)
    shifted = jax.random.randint(jax.random.fold_in(stream_key, 1), (pairs,), 0, 1 << 20) % (slack + 1)
    sizes = sizes.at[1:1 + 2 * pairs:2].set(donor - shifted).at[2:2 + 2 * pairs:2].set(taker + shifted)
    return sizes[jax.random.permutation(jax.random.fold_in(stream_key, 2), number_of)]


def normal_values(key, shape, deviation, reach, split=(), kind=jnp.bfloat16):
    result = jax.random.normal(key, shape, jnp.float32) * deviation
    if len(split) > 0:
        result = steps_of(key, shape, split, -0.22, 0.18) * result
    return jnp.clip(result, min=-reach, max=reach).astype(kind)


def setup_inputs(seed: int = 0) -> dict:
    key_list = jax.random.split(jax.random.key(seed), 17)
    return {
        "tokens": normal_values(key_list[0], (TOKENS, D), 1.0, 6.0, ((0, 8),)),
        "cotangent": normal_values(key_list[1], (TOKENS, D), 1.0, 6.0, ((0, 8),)),
        "lengths": jax.vmap(lambda own: uneven_parts(own, SLOTS, TOK_DEV, LONGEST, 2))(jax.random.split(key_list[2], N_DP)).reshape((N_DP, SLOTS)).astype(jnp.int32),
        "norm_params": draw_norm_params(jax.random.fold_in(key_list[16], 71), 0),
        "joined_weight": normal_values(key_list[4], (D, 3 * D), D ** -0.5, 0.1875, ((1, 4),)),
        "b_qkv": normal_values(key_list[5], (3 * D,), 0.2, 1.25, ((0, 4),)),
        "output_weight": normal_values(key_list[6], (D, D), (D // 32) ** -0.5, 1.0, ((0, 4),)),
        "b_o": normal_values(key_list[7], (D,), 0.2, 1.25),
        "up_weight": normal_values(key_list[8], (D, FF), D ** -0.5, 0.1875, ((1, 4),)),
        "b_up": normal_values(key_list[9], (FF,), 0.2, 1.25, ((0, 4),)),
        "down_weight": normal_values(key_list[10], (FF, D), FF ** -0.5, 0.09375, ((0, 4),)),
        "b_down": normal_values(key_list[11], (D,), 0.2, 1.25),
        "shared_factors": draw_shared_factors(jax.random.fold_in(key_list[16], 71), 0),
        "shared_moments": draw_shared_moments(jax.random.fold_in(key_list[16], 71), 0),
        "local_factors": draw_local_factors(jax.random.fold_in(key_list[16], 71), 0),
        "local_moments": draw_local_moments(jax.random.fold_in(key_list[16], 71), 0),
    }


@jax.custom_vjp
def low(v):
    return lax.optimization_barrier(v.astype(jnp.bfloat16)).astype(jnp.float32)

@jax.custom_vjp
def low_back(v):
    return v

def low_keep(v):
    return (low(v), None)

def low_pass(kept, grad):
    return (grad,)

def back_keep(v):
    return (v, None)

def back_low(kept, grad):
    return (low(grad),)
low.defvjp(low_keep, low_pass)
low_back.defvjp(back_keep, back_low)
first_fix = 1.0 - math.exp(100.0 * math.log(0.9))
second_fix = 1.0 - math.exp(100.0 * math.log(0.999))

def exact_matrix_product(former, latter):
    return jnp.dot(former, latter, precision=lax.Precision.HIGHEST, preferred_element_type=jnp.float32)

def layer_norm(values, gain, shift):
    center = values - lax.optimization_barrier(jnp.mean(values, axis=-1, keepdims=True))
    return center * lax.rsqrt(lax.optimization_barrier(jnp.mean(center * center, axis=-1, keepdims=True)) + 1e-05) * gain + shift

def layout(lengths_row):
    ends = jnp.cumsum(lengths_row).astype(jnp.int32)
    places = jnp.arange(TOK_DEV, dtype=jnp.int32)
    passed = places[:, None] >= ends[None, :]
    doc_ids = lax.optimization_barrier(jnp.sum(passed.astype(jnp.int32), axis=1)).astype(jnp.int32)
    starts = lax.optimization_barrier(jnp.sum(jnp.where(passed, lengths_row[None, :], 0), axis=1)).astype(jnp.int32)
    return (doc_ids, places - starts)

def rotate(values, offsets):
    half = ROT // 2
    freq = 10000.0 ** (-2.0 * jnp.arange(half, dtype=jnp.float32) / ROT)
    angles = offsets.astype(jnp.float32)[:, None] * freq[None, :]
    cosine = jnp.cos(angles)[:, None, :]
    sine = jnp.sin(angles)[:, None, :]
    first = values[..., :half]
    second = values[..., half:ROT]
    return jnp.concatenate([first * cosine - second * sine, second * cosine + first * sine, values[..., ROT:]], axis=-1)

def block_mask(doc_ids, docs_pad, block_start):
    query_docs = lax.dynamic_slice_in_dim(doc_ids, block_start, QB, 0)
    key_docs = lax.dynamic_slice_in_dim(docs_pad, block_start, 3 * QB, 0)
    query_places = block_start + jnp.arange(QB, dtype=jnp.int32)
    key_places = block_start - 2 * QB + jnp.arange(3 * QB, dtype=jnp.int32)
    return (query_docs[:, None] == key_docs[None, :]) & (key_places[None, :] <= query_places[:, None])

def attention(queries, keys, values, doc_ids):
    margin = 2 * QB
    keys_pad = jnp.pad(keys, ((margin, 0), (0, 0), (0, 0)))
    values_pad = jnp.pad(values, ((margin, 0), (0, 0), (0, 0)))
    docs_pad = jnp.concatenate([jnp.full((margin,), -1, jnp.int32), doc_ids])
    score_scale = HD ** (-0.5)

    def block(block_index):
        block_start = block_index * QB
        query_blk = lax.dynamic_slice_in_dim(queries, block_start, QB, 0)
        key_blk = lax.dynamic_slice_in_dim(keys_pad, block_start, 3 * QB, 0)
        value_blk = lax.dynamic_slice_in_dim(values_pad, block_start, 3 * QB, 0)
        allowed = block_mask(doc_ids, docs_pad, block_start)
        scores = low_back(score_scale * jnp.einsum('qhd,khd->hqk', query_blk, key_blk, precision=lax.Precision.HIGHEST))
        scores = jnp.where(allowed[None], scores, -1e+30)
        row_max = lax.optimization_barrier(jnp.max(scores, axis=-1, keepdims=True))
        expo = jnp.exp(scores - row_max)
        probs = low(expo / lax.optimization_barrier(jnp.sum(expo, axis=-1, keepdims=True)))
        return jnp.einsum('hqk,khd->qhd', probs, value_blk, precision=lax.Precision.HIGHEST)
    blocks = lax.map(jax.checkpoint(block), jnp.arange(TOK_DEV // QB, dtype=jnp.int32))
    return blocks.reshape(TOK_DEV, HEADS, HD)

def unpack(local):
    qkv_rows = 3 * D // N_MP
    up_rows = FF // N_MP
    out_rows = D // N_MP
    second_end = qkv_rows + up_rows
    third_end = second_end + out_rows
    query_up_factor = local[:, :qkv_rows].reshape(3 * D, ADAPTER_RANK)
    hidden_up_factor = local[:, qkv_rows:second_end].reshape(FF, ADAPTER_RANK)
    attention_down_factor = local[:, second_end:third_end].reshape(D, ADAPTER_RANK)
    perceptron_down_factor = local[:, third_end:].reshape(FF, ADAPTER_RANK)
    return (query_up_factor, hidden_up_factor, attention_down_factor, perceptron_down_factor)

def forward(x_row, norm_in, shared, local, doc_ids, offsets, frozen_weights):
    query_weight, query_bias_vector, attention_weight, attention_bias_vector, hidden_weight, hidden_bias_vector, perceptron_weight, perceptron_bias_vector = frozen_weights
    adapter_scale = 32.0 / ADAPTER_RANK
    shared_low = low(shared)
    local_low = low(local)
    a_query, a_hidden, attention_up_factor, perceptron_up_factor = (shared_low[0], shared_low[1], shared_low[2], shared_low[3])
    query_up_factor, hidden_up_factor, attention_down_factor, perceptron_down_factor = unpack(local_low)
    attention_normed_input = low(layer_norm(x_row, norm_in[0], norm_in[1]))
    perceptron_normed_input = low(layer_norm(x_row, norm_in[2], norm_in[3]))
    query_low_rank = low(low_back(exact_matrix_product(attention_normed_input, a_query)))
    joined_projection = low_back(exact_matrix_product(attention_normed_input, query_weight) + query_bias_vector + adapter_scale * exact_matrix_product(query_low_rank, query_up_factor.T))
    joined_projection = joined_projection.reshape(TOK_DEV, HEADS, 3, HD)
    queries = low(rotate(joined_projection[:, :, 0], offsets))
    keys = low(rotate(joined_projection[:, :, 1], offsets))
    values = low(joined_projection[:, :, 2])
    mixed_heads = low(low_back(attention(queries, keys, values, doc_ids).reshape(TOK_DEV, D)))
    attention_low_rank = low(low_back(exact_matrix_product(mixed_heads, attention_down_factor)))
    attention_result_rows = exact_matrix_product(mixed_heads, attention_weight) + attention_bias_vector + adapter_scale * exact_matrix_product(attention_low_rank, attention_up_factor.T)
    hidden_low_rank = low(low_back(exact_matrix_product(perceptron_normed_input, a_hidden)))
    hidden_preactivation = low_back(exact_matrix_product(perceptron_normed_input, hidden_weight) + hidden_bias_vector + adapter_scale * exact_matrix_product(hidden_low_rank, hidden_up_factor.T))
    hidden_activations = low(jax.nn.gelu(hidden_preactivation, approximate=False))
    perceptron_low_rank = low(low_back(exact_matrix_product(hidden_activations, perceptron_down_factor)))
    perceptron_result_rows = exact_matrix_product(hidden_activations, perceptron_weight) + perceptron_bias_vector + adapter_scale * exact_matrix_product(perceptron_low_rank, perceptron_up_factor.T)
    return x_row + attention_result_rows + perceptron_result_rows

def adam(param, grad, moments):
    first = 0.9 * moments[0] + 0.1 * grad
    second = 0.999 * moments[1] + 0.001 * grad * grad
    update = first / first_fix / (jnp.sqrt(second / second_fix) + 1e-08)
    return (param - 0.001 * update, jnp.stack([first, second]))

def reference(tokens, cotangent, lengths, norm_params, joined_weight, b_qkv, output_weight, b_o, up_weight, b_up, down_weight, b_down, shared_factors, shared_moments, local_factors, local_moments):
    frozen_weights = tuple((weight.astype(jnp.float32) for weight in (joined_weight, b_qkv, output_weight, b_o, up_weight, b_up, down_weight, b_down)))
    token_rows = tokens.astype(jnp.float32).reshape(N_DP, TOK_DEV, D)
    cot_rows = cotangent.astype(jnp.float32).reshape(N_DP, TOK_DEV, D)

    def one_row(totals, row_item):
        x_row, cot_row, lengths_row = row_item
        doc_ids, offsets = layout(lengths_row)

        def local_forward(x_in, norm_in, shared_in, local_in):
            return forward(x_in, norm_in, shared_in, local_in, doc_ids, offsets, frozen_weights)
        out_row, pull_back = jax.vjp(local_forward, x_row, norm_params, shared_factors, local_factors)
        grad_x, grad_norm, grad_shared, grad_local = pull_back(cot_row)
        totals = (totals[0] + grad_norm, totals[1] + grad_shared, totals[2] + grad_local)
        return (totals, (out_row.astype(jnp.bfloat16), grad_x.astype(jnp.bfloat16)))
    zero_totals = (jnp.zeros_like(norm_params), jnp.zeros_like(shared_factors), jnp.zeros_like(local_factors))
    (norm_grads, shared_grads, local_grads), (out_rows, grad_rows) = lax.scan(one_row, zero_totals, (token_rows, cot_rows, lengths))
    stepped_shared_factors, shared_state = adam(shared_factors, shared_grads, shared_moments)
    new_local, local_state = adam(local_factors, local_grads, local_moments)
    query_up_factor, hidden_up_factor, attention_down_factor, perceptron_down_factor = unpack(new_local)
    adapter_scale = 32.0 / ADAPTER_RANK
    joined_weight_merged = (frozen_weights[0] + adapter_scale * exact_matrix_product(stepped_shared_factors[0], query_up_factor.T)).astype(jnp.bfloat16)
    output_weight_merged = (frozen_weights[2] + adapter_scale * exact_matrix_product(attention_down_factor, stepped_shared_factors[2].T)).astype(jnp.bfloat16)
    up_weight_merged = (frozen_weights[4] + adapter_scale * exact_matrix_product(stepped_shared_factors[1], hidden_up_factor.T)).astype(jnp.bfloat16)
    down_weight_merged = (frozen_weights[6] + adapter_scale * exact_matrix_product(perceptron_down_factor, stepped_shared_factors[3].T)).astype(jnp.bfloat16)
    return (out_rows.reshape(TOKENS, D), grad_rows.reshape(TOKENS, D), norm_grads, shared_grads, local_grads, joined_weight_merged, output_weight_merged, up_weight_merged, down_weight_merged, stepped_shared_factors, new_local, shared_state, local_state)
```

```python
import math

import jax
import jax.numpy as jnp
from jax import lax
from jax.sharding import PartitionSpec as P

HD = 64
ROT = 16
QB = 512


first_fix = 1.0 - math.exp(100.0 * math.log(0.9))
second_fix = 1.0 - math.exp(100.0 * math.log(0.999))


def contract_product(former, latter, former_dim, latter_dim):
    return lax.dot_general(
        former,
        latter,
        (((former_dim,), (latter_dim,)), ((), ())),
        preferred_element_type=jnp.float32,
    )


def normalize(values):
    center = values - jnp.mean(values, axis=-1, keepdims=True)
    inv_std = lax.rsqrt(jnp.mean(center * center, axis=-1, keepdims=True) + 1e-05)
    return (center * inv_std, inv_std)


def layout(lengths_row, token_count):
    ends = jnp.cumsum(lengths_row)
    places = jnp.arange(token_count, dtype=jnp.int32)
    passed = places[:, None] >= ends[None, :]
    doc_ids = jnp.sum(passed.astype(jnp.int32), axis=1)
    starts = jnp.sum(jnp.where(passed, lengths_row[None, :], 0), axis=1)
    return (doc_ids, places - starts)


def rotate(values, offsets):
    half = ROT // 2
    freq = 10000.0 ** (-2.0 * jnp.arange(half, dtype=jnp.float32) / ROT)
    angles = offsets.astype(jnp.float32)[:, None] * freq[None, :]
    cosine = jnp.cos(angles)[:, None, :]
    sine = jnp.sin(angles)[:, None, :]
    first = values[..., :half]
    second = values[..., half:ROT]
    return jnp.concatenate(
        [first * cosine - second * sine, second * cosine + first * sine, values[..., ROT:]], axis=-1
    )


def block_scores(query_blk, key_blk, query_docs, key_docs, query_start, key_start):
    query_places = query_start + jnp.arange(query_blk.shape[0], dtype=jnp.int32)
    key_places = key_start + jnp.arange(key_blk.shape[0], dtype=jnp.int32)
    allowed = (query_docs[:, None] == key_docs[None, :]) & (
        key_places[None, :] <= query_places[:, None]
    )
    scores = HD ** (-0.5) * jnp.einsum(
        "qhd,khd->hqk", query_blk, key_blk, preferred_element_type=jnp.float32
    )
    return jnp.where(allowed[None], scores, -1e30)


def attend_block(queries, keys_rot, values, doc_ids, index):
    start, stop = index * QB, (index + 1) * QB
    low = max(0, start - 2 * QB)
    scores = block_scores(
        queries[start:stop], keys_rot[low:stop], doc_ids[start:stop], doc_ids[low:stop], start, low
    )
    row_max = jnp.max(scores, axis=-1, keepdims=True)
    expo = jnp.exp(scores - row_max)
    row_total = jnp.sum(expo, axis=-1, keepdims=True)
    probs = (expo / row_total).astype(jnp.bfloat16)
    attended = jnp.einsum(
        "hqk,khd->qhd", probs, values[low:stop], preferred_element_type=jnp.float32
    )
    return (attended, row_max + jnp.log(row_total))


def attend_back_block(queries, keys_rot, values, doc_ids, log_sums, grad_blk, index):
    start, stop = index * QB, (index + 1) * QB
    low = max(0, start - 2 * QB)
    query_blk, key_blk, value_blk = queries[start:stop], keys_rot[low:stop], values[low:stop]
    scores = block_scores(
        query_blk, key_blk, doc_ids[start:stop], doc_ids[low:stop], start, low
    )
    probs = jnp.exp(scores - log_sums)
    grad_probs = jnp.einsum("qhd,khd->hqk", grad_blk, value_blk, preferred_element_type=jnp.float32)
    row_dot = jnp.sum(grad_probs * probs, axis=-1, keepdims=True)
    grad_scores = (probs * (grad_probs - row_dot)).astype(jnp.bfloat16)
    query_part = HD ** (-0.5) * jnp.einsum(
        "hqk,khd->qhd", grad_scores, key_blk, preferred_element_type=jnp.float32
    )
    key_part = HD ** (-0.5) * jnp.einsum(
        "hqk,qhd->khd", grad_scores, query_blk, preferred_element_type=jnp.float32
    )
    value_part = jnp.einsum(
        "hqk,qhd->khd", probs.astype(jnp.bfloat16), grad_blk, preferred_element_type=jnp.float32
    )
    return (query_part, key_part, value_part)


def halving_sum(values, axis):
    count = lax.axis_size(axis)
    me = lax.axis_index(axis)
    rest = values.shape[1:]
    rows = values.shape[0] // count
    parts = values.reshape((count, rows) + rest)
    bit = 1
    while bit < count:
        pairs = [(i, i ^ bit) for i in range(count)]
        mine = (me // bit) % 2
        parts = parts.reshape((parts.shape[0] // 2, 2, rows) + rest)
        sent = lax.dynamic_index_in_dim(parts, 1 - mine, 1, keepdims=False)
        kept = lax.dynamic_index_in_dim(parts, mine, 1, keepdims=False)
        parts = kept + lax.ppermute(sent, axis, pairs)
        bit *= 2
    return parts.reshape((rows,) + rest)


def doubling_gather(values, axis):
    count = lax.axis_size(axis)
    me = lax.axis_index(axis)
    rest = values.shape[1:]
    rows = values.shape[0]
    parts = values[None]
    bit = count // 2
    while bit >= 1:
        pairs = [(i, i ^ bit) for i in range(count)]
        mine = (me // bit) % 2
        other = lax.ppermute(parts, axis, pairs)
        low = jnp.where(mine == 0, parts, other)
        high = jnp.where(mine == 0, other, parts)
        parts = jnp.stack([low, high], axis=1).reshape((parts.shape[0] * 2, rows) + rest)
        bit //= 2
    return parts.reshape((count * rows,) + rest)


def line_total(partial, finish):
    count = lax.axis_size("mp")
    me = lax.axis_index("mp")
    half = count // 2
    running = partial
    for k in range(half - 1):
        moved = lax.ppermute(
            running.astype(jnp.bfloat16), "mp", [(k, k + 1), (count - 1 - k, count - 2 - k)]
        )
        running = running + moved.astype(jnp.float32)
    mine = running.astype(jnp.bfloat16)
    other = lax.ppermute(mine, "mp", [(half - 1, half), (half, half - 1)])
    result = finish(mine.astype(jnp.float32) + other.astype(jnp.float32))
    for k in range(half - 2, -1, -1):
        moved = lax.ppermute(result, "mp", [(k + 1, k), (count - 2 - k, count - 1 - k)])
        result = jnp.where((me == k) | (me == count - 1 - k), moved, result)
    return result


def split_rows(block_rows, qkv_cols, hidden_cols, attn_rows):
    second_end = qkv_cols + hidden_cols
    third_end = second_end + attn_rows
    return (
        block_rows[:qkv_cols],
        block_rows[qkv_cols:second_end],
        block_rows[second_end:third_end],
        block_rows[third_end:],
    )


def exact_gelu(values):
    return jax.nn.gelu(values, approximate=False)


def adam(param, grad, moments):
    first = 0.9 * moments[0] + 0.1 * grad
    second = 0.999 * moments[1] + 0.001 * grad * grad
    update = first / first_fix / (jnp.sqrt(second / second_fix) + 1e-08)
    return (param - 0.001 * update, jnp.stack([first, second]))


def per_device(
    tokens,
    cotangent,
    lengths,
    norm_params,
    joined_weight,
    b_qkv,
    output_weight,
    b_o,
    up_weight,
    b_up,
    down_weight,
    b_down,
    shared_factors,
    shared_moments,
    local_factors,
    local_moments,
):
    token_count = tokens.shape[0]
    adapter_rank = shared_factors.shape[2]
    adapter_scale = 32.0 / adapter_rank
    qkv_cols = joined_weight.shape[1]
    hidden_cols = up_weight.shape[1]
    attn_rows = output_weight.shape[0]
    heads_here = qkv_cols // (3 * HD)
    dp_count, mp_count = lax.axis_size("dp"), lax.axis_size("mp")
    blocks = token_count // QB
    doc_ids, offsets = layout(lengths[0], token_count)

    def whole_shared(shards):
        low = doubling_gather(jnp.swapaxes(shards, 0, 1), "mp")
        return jnp.swapaxes(doubling_gather(low, "dp"), 0, 1)

    def whole_local(shard):
        return doubling_gather(shard[0], "dp")

    shared_low = whole_shared(shared_factors.astype(jnp.bfloat16))
    local_low = whole_local(local_factors.astype(jnp.bfloat16))
    a_query, a_hidden, attention_up_factor, perceptron_up_factor = (
        shared_low[0],
        shared_low[1],
        shared_low[2],
        shared_low[3],
    )
    query_up_factor, hidden_up_factor, attention_down_factor, perceptron_down_factor = split_rows(
        local_low, qkv_cols, hidden_cols, attn_rows
    )
    x_in = tokens.astype(jnp.float32)
    hat, inv_std = normalize(x_in)
    attn_in = (hat * norm_params[0] + norm_params[1]).astype(jnp.bfloat16)
    mlp_in = (hat * norm_params[2] + norm_params[3]).astype(jnp.bfloat16)
    query_low_rank = contract_product(attn_in, a_query, 1, 0).astype(jnp.bfloat16)
    joined_projection = (
        contract_product(attn_in, joined_weight, 1, 0)
        + b_qkv.astype(jnp.float32)
        + adapter_scale * contract_product(query_low_rank, query_up_factor, 1, 1)
    )
    joined_projection = joined_projection.reshape(token_count, heads_here, 3, HD)
    queries = rotate(joined_projection[:, :, 0], offsets).astype(jnp.bfloat16)
    keys_rot = rotate(joined_projection[:, :, 1], offsets).astype(jnp.bfloat16)
    values = joined_projection[:, :, 2].astype(jnp.bfloat16)

    hidden_low_rank = contract_product(mlp_in, a_hidden, 1, 0).astype(jnp.bfloat16)
    hidden_preactivation = (
        contract_product(mlp_in, up_weight, 1, 0)
        + b_up.astype(jnp.float32)
        + adapter_scale * contract_product(hidden_low_rank, hidden_up_factor, 1, 1)
    )
    hidden_activations = exact_gelu(hidden_preactivation).astype(jnp.bfloat16)
    mlp_low = contract_product(hidden_activations, perceptron_down_factor, 1, 0).astype(
        jnp.bfloat16
    )
    bias_sum = b_o.astype(jnp.float32) + b_down.astype(jnp.float32)

    mixed_blocks, low_blocks, log_blocks, out_blocks = [], [], [], []
    for index in range(blocks):
        rows = slice(index * QB, (index + 1) * QB)
        attended, log_sums = attend_block(queries, keys_rot, values, doc_ids, index)
        mixed = attended.reshape(QB, heads_here * HD).astype(jnp.bfloat16)
        attn_low = contract_product(mixed, attention_down_factor, 1, 0).astype(jnp.bfloat16)
        partial = (
            contract_product(mixed, output_weight, 1, 0)
            + contract_product(hidden_activations[rows], down_weight, 1, 0)
            + adapter_scale
            * (
                contract_product(attn_low, attention_up_factor, 1, 1)
                + contract_product(mlp_low[rows], perceptron_up_factor, 1, 1)
            )
        )

        def finish_out(total, rows=rows):
            return (x_in[rows] + total + bias_sum).astype(jnp.bfloat16)

        out_blocks.append(line_total(partial, finish_out))
        mixed_blocks.append(mixed)
        low_blocks.append(attn_low)
        log_blocks.append(log_sums)
    out_final = jnp.concatenate(out_blocks, axis=0)
    mixed_heads = jnp.concatenate(mixed_blocks, axis=0)
    attn_low = jnp.concatenate(low_blocks, axis=0)

    attention_low_gradient = (
        adapter_scale * contract_product(cotangent, attention_up_factor, 1, 0)
    ).astype(jnp.bfloat16)
    perceptron_low_gradient = (
        adapter_scale * contract_product(cotangent, perceptron_up_factor, 1, 0)
    ).astype(jnp.bfloat16)
    grad_mixed = (
        contract_product(cotangent, output_weight, 1, 1)
        + contract_product(attention_low_gradient, attention_down_factor, 1, 1)
    ).astype(jnp.bfloat16)
    grad_hidden = contract_product(cotangent, down_weight, 1, 1) + contract_product(
        perceptron_low_gradient, perceptron_down_factor, 1, 1
    )
    gelu_out, gelu_pull = jax.vjp(exact_gelu, hidden_preactivation)
    preactivation_gradient = gelu_pull(grad_hidden)[0].astype(jnp.bfloat16)
    grad_a_attn = contract_product(mixed_heads, attention_low_gradient, 0, 0)
    grad_a_mlp = contract_product(hidden_activations, perceptron_low_gradient, 0, 0)
    hidden_up_gradient = adapter_scale * contract_product(
        preactivation_gradient, hidden_low_rank, 0, 0
    )
    grad_hidden_low = (
        adapter_scale * contract_product(preactivation_gradient, hidden_up_factor, 1, 0)
    ).astype(jnp.bfloat16)
    grad_mlp_part = contract_product(preactivation_gradient, up_weight, 1, 1) + contract_product(
        grad_hidden_low, a_hidden, 1, 1
    )
    grad_a_hidden = contract_product(mlp_in, grad_hidden_low, 0, 0)
    attention_up_gradient = adapter_scale * contract_product(cotangent, attn_low, 0, 0)
    perceptron_up_gradient = adapter_scale * contract_product(cotangent, mlp_low, 0, 0)

    grad_heads = grad_mixed.reshape(token_count, heads_here, HD)
    key_sums = [0.0] * blocks
    value_sums = [0.0] * blocks
    joined_grads, low_grads, grad_blocks = [None] * blocks, [None] * blocks, [None] * blocks
    norm_part = 0.0
    for index in range(blocks - 1, -1, -1):
        rows = slice(index * QB, (index + 1) * QB)
        query_part, key_part, value_part = attend_back_block(
            queries, keys_rot, values, doc_ids, log_blocks[index], grad_heads[rows], index
        )
        low_block = max(0, index - 2)
        for other in range(low_block, index + 1):
            piece = slice((other - low_block) * QB, (other - low_block + 1) * QB)
            key_sums[other] = key_sums[other] + key_part[piece]
            value_sums[other] = value_sums[other] + value_part[piece]
        joined_grad = jnp.stack(
            [
                rotate(query_part, -offsets[rows]),
                rotate(key_sums[index], -offsets[rows]),
                value_sums[index],
            ],
            axis=2,
        )
        joined_grad = joined_grad.reshape(QB, qkv_cols).astype(jnp.bfloat16)
        low_grad = (adapter_scale * contract_product(joined_grad, query_up_factor, 1, 0)).astype(
            jnp.bfloat16
        )
        grad_attn = contract_product(joined_grad, joined_weight, 1, 1) + contract_product(
            low_grad, a_query, 1, 1
        )
        grad_mlp = grad_mlp_part[rows]
        hat_blk = hat[rows]
        norm_part = norm_part + jnp.stack(
            [
                jnp.sum(grad_attn * hat_blk, axis=0),
                jnp.sum(grad_attn, axis=0),
                jnp.sum(grad_mlp * hat_blk, axis=0),
                jnp.sum(grad_mlp, axis=0),
            ]
        )
        scaled = grad_attn * norm_params[0] + grad_mlp * norm_params[2]

        def finish_grad(total, rows=rows, hat_blk=hat_blk):
            spread = total - jnp.mean(total, axis=-1, keepdims=True)
            spread = spread - hat_blk * jnp.mean(total * hat_blk, axis=-1, keepdims=True)
            return (cotangent[rows].astype(jnp.float32) + inv_std[rows] * spread).astype(
                jnp.bfloat16
            )

        grad_blocks[index] = line_total(scaled, finish_grad)
        joined_grads[index] = joined_grad
        low_grads[index] = low_grad
    grad_final = jnp.concatenate(grad_blocks, axis=0)
    joined_rows_gradient = jnp.concatenate(joined_grads, axis=0)
    grad_query_low = jnp.concatenate(low_grads, axis=0)
    query_up_gradient = adapter_scale * contract_product(joined_rows_gradient, query_low_rank, 0, 0)
    grad_a_query = contract_product(attn_in, grad_query_low, 0, 0)

    shard_rows = shared_factors.shape[1]
    shared_part = jnp.stack(
        [grad_a_query, grad_a_hidden, attention_up_gradient, perceptron_up_gradient], axis=1
    )
    norm_columns = jnp.moveaxis(norm_part.reshape(4, -1, shard_rows), 1, 0)
    norm_grads = halving_sum(halving_sum(norm_columns, "dp"), "mp")[0]
    shared_grads = jnp.swapaxes(halving_sum(halving_sum(shared_part, "dp"), "mp"), 0, 1)
    local_part = jnp.concatenate(
        [query_up_gradient, hidden_up_gradient, grad_a_attn, grad_a_mlp], axis=0
    )
    local_grads = halving_sum(local_part, "dp")[None]
    stepped_shared_factors, shared_state = adam(shared_factors, shared_grads, shared_moments)
    new_local, local_state = adam(local_factors, local_grads, local_moments)
    complete_shared_factors = whole_shared(stepped_shared_factors.astype(jnp.bfloat16))
    full_local = whole_local(new_local.astype(jnp.bfloat16))
    updated_query_up, updated_hidden_up, updated_attention_down, updated_perceptron_down = (
        split_rows(full_local, qkv_cols, hidden_cols, attn_rows)
    )
    joined_weight_merged = (
        joined_weight.astype(jnp.float32)
        + adapter_scale * contract_product(complete_shared_factors[0], updated_query_up, 1, 1)
    ).astype(jnp.bfloat16)
    output_weight_merged = (
        output_weight.astype(jnp.float32)
        + adapter_scale
        * contract_product(updated_attention_down, complete_shared_factors[2], 1, 1)
    ).astype(jnp.bfloat16)
    up_weight_merged = (
        up_weight.astype(jnp.float32)
        + adapter_scale
        * contract_product(complete_shared_factors[1], updated_hidden_up, 1, 1)
    ).astype(jnp.bfloat16)
    down_weight_merged = (
        down_weight.astype(jnp.float32)
        + adapter_scale
        * contract_product(updated_perceptron_down, complete_shared_factors[3], 1, 1)
    ).astype(jnp.bfloat16)
    return (
        out_final,
        grad_final,
        norm_grads,
        shared_grads,
        local_grads,
        joined_weight_merged,
        output_weight_merged,
        up_weight_merged,
        down_weight_merged,
        stepped_shared_factors,
        new_local,
        shared_state,
        local_state,
    )


def solution(mesh):
    placed = (
        P("dp", None),
        P("dp", None),
        P("dp", None),
        P(),
        P(None, "mp"),
        P("mp"),
        P("mp", None),
        P(),
        P(None, "mp"),
        P("mp"),
        P("mp", None),
        P(),
        P(None, ("dp", "mp"), None),
        P(None, None, ("dp", "mp"), None),
        P("mp", "dp", None),
        P(None, "mp", "dp", None),
    )
    return jax.shard_map(
        per_device,
        mesh=mesh,
        in_specs=placed,
        out_specs=(
            P("dp", None),
            P("dp", None),
            P(None, ("dp", "mp")),
            P(None, ("dp", "mp"), None),
            P("mp", "dp", None),
            P(None, "mp"),
            P("mp", None),
            P(None, "mp"),
            P("mp", None),
            P(None, ("dp", "mp"), None),
            P("mp", "dp", None),
            P(None, None, ("dp", "mp"), None),
            P(None, "mp", "dp", None),
        ),
        check_vma=False,
    )
```

```python
import functools
import math

import jax
import jax.numpy as jnp
from jax import lax
from jax.experimental import pallas as pl
from jax.experimental.pallas import tpu as pltpu
from jax.sharding import PartitionSpec as P


HD = 64
ROT = 16
QB = 512


first_fix = 1.0 - math.exp(100.0 * math.log(0.9))
second_fix = 1.0 - math.exp(100.0 * math.log(0.999))


def contract_product(former, latter, former_dim, latter_dim):
    return lax.dot_general(
        former,
        latter,
        (((former_dim,), (latter_dim,)), ((), ())),
        preferred_element_type=jnp.float32,
    )


def normalize(values):
    center = values - jnp.mean(values, axis=-1, keepdims=True)
    inv_std = lax.rsqrt(jnp.mean(center * center, axis=-1, keepdims=True) + 1e-05)
    return (center * inv_std, inv_std)


def layout(lengths_row, token_count):
    ends = jnp.cumsum(lengths_row)
    places = jnp.arange(token_count, dtype=jnp.int32)
    passed = places[:, None] >= ends[None, :]
    doc_ids = jnp.sum(passed.astype(jnp.int32), axis=1)
    starts = jnp.sum(jnp.where(passed, lengths_row[None, :], 0), axis=1)
    return (doc_ids, places - starts)


def rotary_tables(offsets):
    half = ROT // 2
    freq = 10000.0 ** (-2.0 * jnp.arange(half, dtype=jnp.float32) / ROT)
    angles = freq[:, None] * offsets.astype(jnp.float32)[None, :]
    cosine, sine = jnp.cos(angles), jnp.sin(angles)
    rest = HD - ROT
    cosine = jnp.concatenate([cosine, cosine, jnp.ones((rest, offsets.shape[0]))], axis=0)
    sine = jnp.concatenate([sine, sine, jnp.zeros((rest, offsets.shape[0]))], axis=0)
    return (cosine.T, sine.T)


def turn_matrix():
    rows = lax.broadcasted_iota(jnp.int32, (HD, HD), 0)
    cols = lax.broadcasted_iota(jnp.int32, (HD, HD), 1)
    half = ROT // 2
    back = (rows == cols + half) & (cols < half)
    fore = (rows + half == cols) & (cols < ROT)
    return jnp.where(fore, 1.0, 0.0) - jnp.where(back, 1.0, 0.0)


def turned(values, cosine, sine, turn):
    swapped = jnp.dot(
        values, turn, precision=lax.Precision.HIGHEST, preferred_element_type=jnp.float32
    )
    return values * cosine + swapped * sine


def prepare_kernel(
    joined_ref, mixed_ref, cos_ref, sin_ref, q_ref, k_ref, v_ref, g_ref, kt_ref, vt_ref
):
    cosine, sine, turn = cos_ref[...], sin_ref[...], turn_matrix()
    for head in range(q_ref.shape[0]):
        base = head * 3 * HD
        query = turned(joined_ref[:, base : base + HD], cosine, sine, turn)
        key = turned(joined_ref[:, base + HD : base + 2 * HD], cosine, sine, turn)
        value = joined_ref[:, base + 2 * HD : base + 3 * HD]
        q_ref[head] = (query * HD ** (-0.5)).astype(jnp.bfloat16)
        k_ref[head] = key.astype(jnp.bfloat16)
        v_ref[head] = value.astype(jnp.bfloat16)
        kt_ref[head] = key.T.astype(jnp.bfloat16)
        vt_ref[head] = value.T.astype(jnp.bfloat16)
        g_ref[head] = mixed_ref[:, head * HD : (head + 1) * HD]


def prepare(joined, grad_mixed, cosine, sine):
    count, heads = joined.shape[0], joined.shape[1] // (3 * HD)
    tall = jax.ShapeDtypeStruct((heads, count, HD), jnp.bfloat16)
    wide = jax.ShapeDtypeStruct((heads, HD, count), jnp.bfloat16)
    tall_spec = pl.BlockSpec((heads, QB, HD), lambda i: (0, i, 0))
    wide_spec = pl.BlockSpec((heads, HD, QB), lambda i: (0, 0, i))

    def rows(width):
        return pl.BlockSpec((QB, width), lambda i: (i, 0))

    return pl.pallas_call(
        prepare_kernel,
        grid=(count // QB,),
        in_specs=[rows(heads * 3 * HD), rows(heads * HD), rows(HD), rows(HD)],
        out_specs=[tall_spec] * 4 + [wide_spec] * 2,
        out_shape=[tall] * 4 + [wide] * 2,
        name="prepare",
    )(joined, grad_mixed, cosine, sine)


SUB = 256


def attention_kernel(index, *refs):
    has_in, has_out = index[1], index[0] > 0
    chunk = index[0]
    refs = list(refs)
    q_ref, g_ref, k_ref, v_ref, kt_ref, vt_ref, col_ref, row_ref, cos_ref, sin_ref = refs[:10]
    refs = refs[10:]
    if has_in:
        dk_in, dv_in = refs[:2]
        refs = refs[2:]
    mix_ref, joined_ref = refs[:2]
    refs = refs[2:]
    if has_out:
        dk_out, dv_out = refs[:2]
        refs = refs[2:]
    dk_acc, dv_acc, dq_acc, bias_ref = refs
    low, stop = max(0, chunk - 2) * QB, (chunk + 1) * QB
    size = stop - low
    dk_acc[...] = jnp.zeros(dk_acc.shape, jnp.float32)
    dv_acc[...] = jnp.zeros(dv_acc.shape, jnp.float32)
    if has_in:
        first = max(0, chunk - 1) * QB - low
        dk_acc[:, first:size] = dk_in[...]
        dv_acc[:, first:size] = dv_in[...]
    for part in range(QB // SUB):
        here = chunk * QB + part * SUB
        left = max(0, here - 2 * QB)
        width = here + SUB - left
        rel = left - low
        own = slice(part * SUB, (part + 1) * SUB)
        places = left + lax.broadcasted_iota(jnp.int32, (width, SUB), 0)
        mine = here + lax.broadcasted_iota(jnp.int32, (width, SUB), 1)
        allowed = (col_ref[left : left + width] == row_ref[:, here : here + SUB]) & (
            places <= mine
        )
        bias_ref[:width] = jnp.where(allowed, 0.0, -1e30)
        for head in range(2):
            query, grad = q_ref[head, own], g_ref[head, own]
            key, value = k_ref[head, left : left + width], v_ref[head, left : left + width]
            scores = contract_product(key, query, 1, 1) + bias_ref[:width]
            expo = jnp.exp(scores - jnp.max(scores, axis=0, keepdims=True))
            probs = expo * (1.0 / jnp.sum(expo, axis=0, keepdims=True))
            low_probs = probs.astype(jnp.bfloat16)
            mixed = contract_product(vt_ref[head, :, left : left + width], low_probs, 1, 0)
            mix_ref[head * HD : (head + 1) * HD, own] = mixed.astype(jnp.bfloat16)
            grad_probs = contract_product(value, grad, 1, 1)
            dots = jnp.sum(grad_probs * probs, axis=0, keepdims=True)
            grad_scores = (probs * (grad_probs - dots)).astype(jnp.bfloat16)
            dk_acc[head, rel : rel + width] += contract_product(grad_scores, query, 1, 0)
            dv_acc[head, rel : rel + width] += contract_product(low_probs, grad, 1, 0)
            grad_query = contract_product(kt_ref[head, :, left : left + width], grad_scores, 1, 0)
            dq_acc[head, own] = (HD ** (-0.5) * grad_query).T
    cosine, sine, turn = cos_ref[...], -sin_ref[...], turn_matrix()
    for head in range(2):
        base = head * 3 * HD
        grad_query = turned(dq_acc[head], cosine, sine, turn)
        grad_key = turned(dk_acc[head, size - QB : size], cosine, sine, turn)
        joined_ref[:, base : base + HD] = grad_query.astype(jnp.bfloat16)
        joined_ref[:, base + HD : base + 2 * HD] = grad_key.astype(jnp.bfloat16)
        joined_ref[:, base + 2 * HD : base + 3 * HD] = dv_acc[head, size - QB : size].astype(
            jnp.bfloat16
        )
    if has_out:
        dk_out[...] = dk_acc[:, : size - QB]
        dv_out[...] = dv_acc[:, : size - QB]


def attention_chunk(chunk, pieces, doc_ids, cosine, sine, carry):
    queries, keys, values, grads, keys_turned, values_turned = pieces
    heads, count, _ = queries.shape
    low, stop = max(0, chunk - 2) * QB, (chunk + 1) * QB
    size = stop - low
    own = pl.BlockSpec((2, QB, HD), lambda h: (h, chunk, 0))
    tall = pl.BlockSpec((2, count, HD), lambda h: (h, 0, 0))
    wide = pl.BlockSpec((2, HD, count), lambda h: (h, 0, 0))
    table = pl.BlockSpec((QB, HD), lambda h: (chunk, 0))
    in_specs = [
        own,
        own,
        tall,
        tall,
        wide,
        wide,
        pl.BlockSpec((count, 1), lambda h: (0, 0)),
        pl.BlockSpec((1, count), lambda h: (0, 0)),
        table,
        table,
    ]
    operands = [
        queries,
        grads,
        keys,
        values,
        keys_turned,
        values_turned,
        doc_ids[:, None],
        doc_ids[None, :],
        cosine,
        sine,
    ]
    if carry is not None:
        in_specs += [pl.BlockSpec((2, carry[0].shape[1], HD), lambda h: (h, 0, 0))] * 2
        operands += list(carry)
    out_specs = [
        pl.BlockSpec((2 * HD, QB), lambda h: (h, 0)),
        pl.BlockSpec((QB, 6 * HD), lambda h: (0, h)),
    ]
    out_shape = [
        jax.ShapeDtypeStruct((heads * HD, QB), jnp.bfloat16),
        jax.ShapeDtypeStruct((QB, heads * 3 * HD), jnp.bfloat16),
    ]
    if chunk > 0:
        out_specs += [pl.BlockSpec((2, size - QB, HD), lambda h: (h, 0, 0))] * 2
        out_shape += [jax.ShapeDtypeStruct((heads, size - QB, HD), jnp.float32)] * 2
    results = pl.pallas_call(
        functools.partial(attention_kernel, (chunk, carry is not None)),
        grid=(heads // 2,),
        in_specs=in_specs,
        out_specs=out_specs,
        out_shape=out_shape,
        scratch_shapes=[
            pltpu.VMEM((2, size, HD), jnp.float32),
            pltpu.VMEM((2, size, HD), jnp.float32),
            pltpu.VMEM((2, QB, HD), jnp.float32),
            pltpu.VMEM((2 * QB + SUB, SUB), jnp.float32),
        ],
        compiler_params=pltpu.CompilerParams(vmem_limit_bytes=40 * 2**20),
    )(*operands)
    return results[0], results[1], tuple(results[2:])


def erf(values):
    return lax.erf(values)


def perceptron_kernel(
    scale,
    in_ref,
    dy_ref,
    up_ref,
    down_ref,
    low_ref,
    up_factor_ref,
    grad_low_ref,
    down_factor_ref,
    bias_ref,
    b_down_ref,
    a_up_ref,
    hidden_ref,
    grad_pre_ref,
    out_ref,
    grad_ref,
    down_low_ref,
    up_low_ref,
    out_acc,
    grad_acc,
    down_acc,
    up_acc,
):
    step = pl.program_id(0)

    @pl.when(step == 0)
    def _():
        for ref in (out_acc, grad_acc, down_acc, up_acc):
            ref[...] = jnp.zeros(ref.shape, jnp.float32)

    pre = (
        contract_product(in_ref[...], up_ref[...], 1, 0)
        + scale * contract_product(low_ref[...], up_factor_ref[...], 1, 1)
        + bias_ref[...]
    )
    density = 0.5 * (1.0 + erf(pre * math.sqrt(0.5)))
    hidden = (pre * density).astype(jnp.bfloat16)
    slope = density + pre * (jnp.exp(-0.5 * pre * pre) * (1.0 / math.sqrt(2.0 * math.pi)))
    grad_hidden = contract_product(dy_ref[...], down_ref[...], 1, 1) + contract_product(
        grad_low_ref[...], down_factor_ref[...], 1, 1
    )
    grad_pre = (grad_hidden * slope).astype(jnp.bfloat16)
    hidden_ref[...] = hidden
    grad_pre_ref[...] = grad_pre
    out_acc[...] += contract_product(hidden, down_ref[...], 1, 0)
    down_acc[...] += contract_product(hidden, down_factor_ref[...], 1, 0)
    grad_acc[...] += contract_product(grad_pre, up_ref[...], 1, 1)
    up_acc[...] += contract_product(grad_pre, up_factor_ref[...], 1, 0)

    @pl.when(step == pl.num_programs(0) - 1)
    def _():
        down_low = down_acc[...].astype(jnp.bfloat16)
        up_low = (scale * up_acc[...]).astype(jnp.bfloat16)
        down_low_ref[...] = down_low
        up_low_ref[...] = up_low
        out_ref[...] = out_acc[...] + scale * contract_product(down_low, b_down_ref[...], 1, 1)
        grad_ref[...] = grad_acc[...] + contract_product(up_low, a_up_ref[...], 1, 1)


def perceptron_chunk(chunk, scale, row_arrays, weights):
    mlp_in, cotangent, low_rank, grad_low = row_arrays
    up_weight, down_weight, up_factor, down_factor, bias, b_factor, a_factor = weights
    width, hidden = up_weight.shape
    rank = up_factor.shape[1]
    cols = min(256, hidden)

    def rows(size):
        return pl.BlockSpec((QB, size), lambda j: (chunk, 0))

    def whole(shape):
        return pl.BlockSpec(shape, lambda j: (0, 0))

    return pl.pallas_call(
        functools.partial(perceptron_kernel, scale),
        grid=(hidden // cols,),
        in_specs=[
            rows(width),
            rows(width),
            pl.BlockSpec((width, cols), lambda j: (0, j)),
            pl.BlockSpec((cols, width), lambda j: (j, 0)),
            rows(rank),
            pl.BlockSpec((cols, rank), lambda j: (j, 0)),
            rows(rank),
            pl.BlockSpec((cols, rank), lambda j: (j, 0)),
            pl.BlockSpec((1, cols), lambda j: (0, j)),
            whole((width, rank)),
            whole((width, rank)),
        ],
        out_specs=[
            pl.BlockSpec((QB, cols), lambda j: (0, j)),
            pl.BlockSpec((QB, cols), lambda j: (0, j)),
            whole((QB, width)),
            whole((QB, width)),
            whole((QB, rank)),
            whole((QB, rank)),
        ],
        out_shape=[
            jax.ShapeDtypeStruct((QB, hidden), jnp.bfloat16),
            jax.ShapeDtypeStruct((QB, hidden), jnp.bfloat16),
            jax.ShapeDtypeStruct((QB, width), jnp.float32),
            jax.ShapeDtypeStruct((QB, width), jnp.float32),
            jax.ShapeDtypeStruct((QB, rank), jnp.bfloat16),
            jax.ShapeDtypeStruct((QB, rank), jnp.bfloat16),
        ],
        scratch_shapes=[
            pltpu.VMEM((QB, width), jnp.float32),
            pltpu.VMEM((QB, width), jnp.float32),
            pltpu.VMEM((QB, rank), jnp.float32),
            pltpu.VMEM((QB, rank), jnp.float32),
        ],
        compiler_params=pltpu.CompilerParams(vmem_limit_bytes=40 * 2**20),
    )(
        mlp_in,
        cotangent,
        up_weight,
        down_weight,
        low_rank,
        up_factor,
        grad_low,
        down_factor,
        bias,
        b_factor,
        a_factor,
    )


def partial_kernel(
    scale,
    mixed_ref,
    joined_ref,
    mlp_out_ref,
    mlp_grad_ref,
    hat_ref,
    norm_ref,
    output_ref,
    weight_ref,
    a_o_ref,
    b_o_ref,
    b_qkv_ref,
    a_qkv_ref,
    out_ref,
    grad_ref,
    low_ref,
    grad_low_ref,
    sums_ref,
):
    mixed, joined, hat = mixed_ref[...], joined_ref[...], hat_ref[...]
    low = contract_product(mixed, a_o_ref[...], 0, 0).astype(jnp.bfloat16)
    low_ref[...] = low
    out_ref[...] = (
        mlp_out_ref[...]
        + contract_product(mixed, output_ref[...], 0, 0)
        + scale * contract_product(low, b_o_ref[...], 1, 1)
    ).astype(jnp.bfloat16)
    grad_low = (scale * contract_product(joined, b_qkv_ref[...], 1, 0)).astype(jnp.bfloat16)
    grad_low_ref[...] = grad_low
    grad_attn = contract_product(joined, weight_ref[...], 1, 1) + contract_product(
        grad_low, a_qkv_ref[...], 1, 1
    )
    grad_mlp = mlp_grad_ref[...]
    grad_ref[...] = (grad_attn * norm_ref[0:1] + grad_mlp * norm_ref[2:3]).astype(jnp.bfloat16)
    sums = [
        jnp.sum(grad_attn * hat, axis=0, keepdims=True),
        jnp.sum(grad_attn, axis=0, keepdims=True),
        jnp.sum(grad_mlp * hat, axis=0, keepdims=True),
        jnp.sum(grad_mlp, axis=0, keepdims=True),
    ]

    @pl.when(pl.program_id(0) == 0)
    def _():
        sums_ref[...] = jnp.zeros(sums_ref.shape, jnp.float32)

    for row in range(4):
        sums_ref[row : row + 1] += sums[row]


def partial_chunk(chunk, scale, mixed, joined, mlp_out, mlp_grad, hat, norm_params, weights):
    width = mlp_out.shape[1]
    rank = weights[2].shape[1]
    step = 128
    steps = QB // step

    def rows(size):
        return pl.BlockSpec((step, size), lambda i: (i, 0))

    def whole(array):
        return pl.BlockSpec(array.shape, lambda i: (0, 0))

    return pl.pallas_call(
        functools.partial(partial_kernel, scale),
        grid=(steps,),
        in_specs=[
            pl.BlockSpec((mixed.shape[0], step), lambda i: (0, i)),
            rows(joined.shape[1]),
            rows(width),
            rows(width),
            pl.BlockSpec((step, width), lambda i: (chunk * steps + i, 0)),
            whole(norm_params),
        ]
        + [whole(weight) for weight in weights],
        out_specs=[
            rows(width),
            rows(width),
            rows(rank),
            rows(rank),
            pl.BlockSpec((8, width), lambda i: (0, 0)),
        ],
        out_shape=[
            jax.ShapeDtypeStruct((QB, width), jnp.bfloat16),
            jax.ShapeDtypeStruct((QB, width), jnp.bfloat16),
            jax.ShapeDtypeStruct((QB, rank), jnp.bfloat16),
            jax.ShapeDtypeStruct((QB, rank), jnp.bfloat16),
            jax.ShapeDtypeStruct((8, width), jnp.float32),
        ],
        compiler_params=pltpu.CompilerParams(vmem_limit_bytes=40 * 2**20),
    )(mixed, joined, mlp_out, mlp_grad, hat, norm_params, *weights)


def halving_sum(values, axis):
    count = lax.axis_size(axis)
    me = lax.axis_index(axis)
    rest = values.shape[1:]
    rows = values.shape[0] // count
    parts = values.reshape((count, rows) + rest)
    bit = 1
    while bit < count:
        pairs = [(i, i ^ bit) for i in range(count)]
        mine = (me // bit) % 2
        parts = parts.reshape((parts.shape[0] // 2, 2, rows) + rest)
        sent = lax.dynamic_index_in_dim(parts, 1 - mine, 1, keepdims=False)
        kept = lax.dynamic_index_in_dim(parts, mine, 1, keepdims=False)
        parts = kept + lax.ppermute(sent, axis, pairs)
        bit *= 2
    return parts.reshape((rows,) + rest)


def doubling_gather(values, axis):
    count = lax.axis_size(axis)
    me = lax.axis_index(axis)
    rest = values.shape[1:]
    rows = values.shape[0]
    parts = values[None]
    bit = count // 2
    while bit >= 1:
        pairs = [(i, i ^ bit) for i in range(count)]
        mine = (me // bit) % 2
        other = lax.ppermute(parts, axis, pairs)
        low = jnp.where(mine == 0, parts, other)
        high = jnp.where(mine == 0, other, parts)
        parts = jnp.stack([low, high], axis=1).reshape((parts.shape[0] * 2, rows) + rest)
        bit //= 2
    return parts.reshape((count * rows,) + rest)


def added(first, second):
    return first.astype(jnp.float32) + second.astype(jnp.float32)


def small_call(kernel, size, operands, specs, steps):
    width = operands[0].shape[1]
    return pl.pallas_call(
        kernel,
        grid=(steps,),
        in_specs=specs,
        out_specs=pl.BlockSpec((size, width), lambda i: (i, 0)),
        out_shape=jax.ShapeDtypeStruct((size * steps, width), jnp.bfloat16),
    )(*operands)


def row_specs(size, width, first=0):
    return pl.BlockSpec((size, width), lambda i: (first + i, 0))


def add_kernel(first_ref, second_ref, out_ref):
    out_ref[...] = added(first_ref[...], second_ref[...]).astype(jnp.bfloat16)


def add_rows(first, second):
    count, width = first.shape
    size = 128
    return small_call(
        add_kernel, size, (first, second), [row_specs(size, width)] * 2, count // size
    )


def finish_out_kernel(first_ref, second_ref, token_ref, bias_ref, out_ref):
    total = added(first_ref[...], second_ref[...])
    out_ref[...] = (token_ref[...].astype(jnp.float32) + total + bias_ref[...]).astype(
        jnp.bfloat16
    )


def finish_out(first, second, tokens, bias, start):
    count, width = first.shape
    size = 128
    specs = [row_specs(size, width)] * 2 + [
        row_specs(size, width, start // size),
        pl.BlockSpec((1, width), lambda i: (0, 0)),
    ]
    return small_call(finish_out_kernel, size, (first, second, tokens, bias), specs, count // size)


def finish_grad_kernel(first_ref, second_ref, dy_ref, hat_ref, std_ref, out_ref):
    total, hat = added(first_ref[...], second_ref[...]), hat_ref[...]
    spread = total - jnp.mean(total, axis=-1, keepdims=True)
    spread = spread - hat * jnp.mean(total * hat, axis=-1, keepdims=True)
    out_ref[...] = (dy_ref[...].astype(jnp.float32) + std_ref[...] * spread).astype(jnp.bfloat16)


def finish_grad(first, second, cotangent, hat, inv_std, start):
    count, width = first.shape
    size = 128
    late = row_specs(size, width, start // size)
    specs = [row_specs(size, width)] * 2 + [late, late, row_specs(size, 1, start // size)]
    return small_call(
        finish_grad_kernel, size, (first, second, cotangent, hat, inv_std), specs, count // size
    )


def line_total(partial, finish):
    count = lax.axis_size("mp")
    me = lax.axis_index("mp")
    half = count // 2
    running = partial
    for k in range(half - 1):
        moved = lax.ppermute(running, "mp", [(k, k + 1), (count - 1 - k, count - 2 - k)])
        running = add_rows(running, moved)
    other = lax.ppermute(running, "mp", [(half - 1, half), (half, half - 1)])
    result = finish(running, other)
    for k in range(half - 2, -1, -1):
        moved = lax.ppermute(result, "mp", [(k + 1, k), (count - 2 - k, count - 1 - k)])
        result = jnp.where((me == k) | (me == count - 1 - k), moved, result)
    return result


def split_rows(block_rows, qkv_cols, hidden_cols, attn_rows):
    second_end = qkv_cols + hidden_cols
    third_end = second_end + attn_rows
    return (
        block_rows[:qkv_cols],
        block_rows[qkv_cols:second_end],
        block_rows[second_end:third_end],
        block_rows[third_end:],
    )


def adam(param, grad, moments):
    first = 0.9 * moments[0] + 0.1 * grad
    second = 0.999 * moments[1] + 0.001 * grad * grad
    update = first / first_fix / (jnp.sqrt(second / second_fix) + 1e-08)
    return (param - 0.001 * update, jnp.stack([first, second]))


def per_device(
    tokens,
    cotangent,
    lengths,
    norm_params,
    joined_weight,
    b_qkv,
    output_weight,
    b_o,
    up_weight,
    b_up,
    down_weight,
    b_down,
    shared_factors,
    shared_moments,
    local_factors,
    local_moments,
):
    token_count = tokens.shape[0]
    adapter_rank = shared_factors.shape[2]
    adapter_scale = 32.0 / adapter_rank
    qkv_cols = joined_weight.shape[1]
    hidden_cols = up_weight.shape[1]
    attn_rows = output_weight.shape[0]
    blocks = token_count // QB
    doc_ids, offsets = layout(lengths[0], token_count)
    cosine, sine = rotary_tables(offsets)

    def whole_shared(shards):
        low = doubling_gather(jnp.swapaxes(shards, 0, 1), "mp")
        return jnp.swapaxes(doubling_gather(low, "dp"), 0, 1)

    def whole_local(shard):
        return doubling_gather(shard[0], "dp")

    shared_low = whole_shared(shared_factors.astype(jnp.bfloat16))
    local_low = whole_local(local_factors.astype(jnp.bfloat16))
    a_query, a_hidden, attention_up_factor, perceptron_up_factor = (
        shared_low[0],
        shared_low[1],
        shared_low[2],
        shared_low[3],
    )
    query_up_factor, hidden_up_factor, attention_down_factor, perceptron_down_factor = split_rows(
        local_low, qkv_cols, hidden_cols, attn_rows
    )
    x_in = tokens.astype(jnp.float32)
    hat, inv_std = normalize(x_in)
    attn_in = (hat * norm_params[0] + norm_params[1]).astype(jnp.bfloat16)
    mlp_in = (hat * norm_params[2] + norm_params[3]).astype(jnp.bfloat16)
    query_low_rank = contract_product(attn_in, a_query, 1, 0).astype(jnp.bfloat16)
    joined_projection = (
        contract_product(attn_in, joined_weight, 1, 0)
        + b_qkv.astype(jnp.float32)
        + adapter_scale * contract_product(query_low_rank, query_up_factor, 1, 1)
    )
    hidden_low_rank = contract_product(mlp_in, a_hidden, 1, 0).astype(jnp.bfloat16)
    bias_sum = b_o.astype(jnp.float32) + b_down.astype(jnp.float32)

    attention_low_gradient = (
        adapter_scale * contract_product(cotangent, attention_up_factor, 1, 0)
    ).astype(jnp.bfloat16)
    perceptron_low_gradient = (
        adapter_scale * contract_product(cotangent, perceptron_up_factor, 1, 0)
    ).astype(jnp.bfloat16)
    grad_mixed = (
        contract_product(cotangent, output_weight, 1, 1)
        + contract_product(attention_low_gradient, attention_down_factor, 1, 1)
    ).astype(jnp.bfloat16)
    pieces = prepare(joined_projection, grad_mixed, cosine, sine)
    mlp_weights = (
        up_weight,
        down_weight,
        hidden_up_factor,
        perceptron_down_factor,
        b_up.astype(jnp.float32)[None],
        perceptron_up_factor,
        a_hidden,
    )
    attention_weights = (
        output_weight,
        joined_weight,
        attention_down_factor,
        attention_up_factor,
        query_up_factor,
        a_query,
    )
    mlp_rows = (mlp_in, cotangent, hidden_low_rank, perceptron_low_gradient)
    carry = None
    made = [None] * blocks
    norm_part = 0.0
    for index in range(blocks - 1, -1, -1):
        mlp_made = perceptron_chunk(index, adapter_scale, mlp_rows, mlp_weights)
        mixed, joined_grad, carry = attention_chunk(
            index, pieces, doc_ids, cosine, sine, carry
        )
        hidden, grad_pre, mlp_out, mlp_grad, mlp_low, hidden_grad_low = mlp_made
        out_part, grad_part, attn_low, query_grad_low, sums = partial_chunk(
            index,
            adapter_scale,
            mixed,
            joined_grad,
            mlp_out,
            mlp_grad,
            hat,
            norm_params,
            attention_weights,
        )
        norm_part = norm_part + sums[:4]
        count = 2 if index == 0 else 1
        size = QB // count
        outs, grads = [], []
        for piece in range(count):
            start = index * QB + piece * size
            inner = slice(piece * size, (piece + 1) * size)

            def end_out(first, second, start=start):
                return finish_out(first, second, tokens, bias_sum[None], start)

            def end_grad(first, second, start=start):
                return finish_grad(first, second, cotangent, hat, inv_std, start)

            grads.append(line_total(grad_part[inner], end_grad))
            outs.append(line_total(out_part[inner], end_out))
        made[index] = (
            mixed,
            hidden,
            grad_pre,
            joined_grad,
            attn_low,
            mlp_low,
            query_grad_low,
            hidden_grad_low,
            jnp.concatenate(outs, axis=0) if count > 1 else outs[0],
            jnp.concatenate(grads, axis=0) if count > 1 else grads[0],
        )

    def joined_up(place, axis=0):
        return jnp.concatenate([made[index][place] for index in range(blocks)], axis=axis)

    mixed_turned = joined_up(0, 1)
    hidden_activations, preactivation_gradient, joined_rows_gradient = (
        joined_up(1),
        joined_up(2),
        joined_up(3),
    )
    attn_low, mlp_low, grad_query_low, grad_hidden_low = (
        joined_up(4),
        joined_up(5),
        joined_up(6),
        joined_up(7),
    )
    out_final, grad_final = joined_up(8), joined_up(9)
    grad_a_attn = contract_product(mixed_turned, attention_low_gradient, 1, 0)
    grad_a_mlp = contract_product(hidden_activations, perceptron_low_gradient, 0, 0)
    hidden_up_gradient = adapter_scale * contract_product(
        preactivation_gradient, hidden_low_rank, 0, 0
    )
    grad_a_hidden = contract_product(mlp_in, grad_hidden_low, 0, 0)
    attention_up_gradient = adapter_scale * contract_product(cotangent, attn_low, 0, 0)
    perceptron_up_gradient = adapter_scale * contract_product(cotangent, mlp_low, 0, 0)
    query_up_gradient = adapter_scale * contract_product(joined_rows_gradient, query_low_rank, 0, 0)
    grad_a_query = contract_product(attn_in, grad_query_low, 0, 0)

    shard_rows = shared_factors.shape[1]
    shared_part = jnp.stack(
        [grad_a_query, grad_a_hidden, attention_up_gradient, perceptron_up_gradient], axis=1
    )
    norm_columns = jnp.moveaxis(norm_part.reshape(4, -1, shard_rows), 1, 0)
    norm_grads = halving_sum(halving_sum(norm_columns, "dp"), "mp")[0]
    shared_grads = jnp.swapaxes(halving_sum(halving_sum(shared_part, "dp"), "mp"), 0, 1)
    local_part = jnp.concatenate(
        [query_up_gradient, hidden_up_gradient, grad_a_attn, grad_a_mlp], axis=0
    )
    local_grads = halving_sum(local_part, "dp")[None]
    stepped_shared_factors, shared_state = adam(shared_factors, shared_grads, shared_moments)
    new_local, local_state = adam(local_factors, local_grads, local_moments)
    complete_shared_factors = whole_shared(stepped_shared_factors.astype(jnp.bfloat16))
    full_local = whole_local(new_local.astype(jnp.bfloat16))
    updated_query_up, updated_hidden_up, updated_attention_down, updated_perceptron_down = (
        split_rows(full_local, qkv_cols, hidden_cols, attn_rows)
    )
    joined_weight_merged = (
        joined_weight.astype(jnp.float32)
        + adapter_scale * contract_product(complete_shared_factors[0], updated_query_up, 1, 1)
    ).astype(jnp.bfloat16)
    output_weight_merged = (
        output_weight.astype(jnp.float32)
        + adapter_scale
        * contract_product(updated_attention_down, complete_shared_factors[2], 1, 1)
    ).astype(jnp.bfloat16)
    up_weight_merged = (
        up_weight.astype(jnp.float32)
        + adapter_scale
        * contract_product(complete_shared_factors[1], updated_hidden_up, 1, 1)
    ).astype(jnp.bfloat16)
    down_weight_merged = (
        down_weight.astype(jnp.float32)
        + adapter_scale
        * contract_product(updated_perceptron_down, complete_shared_factors[3], 1, 1)
    ).astype(jnp.bfloat16)
    return (
        out_final,
        grad_final,
        norm_grads,
        shared_grads,
        local_grads,
        joined_weight_merged,
        output_weight_merged,
        up_weight_merged,
        down_weight_merged,
        stepped_shared_factors,
        new_local,
        shared_state,
        local_state,
    )


def solution(mesh):
    placed = (
        P("dp", None),
        P("dp", None),
        P("dp", None),
        P(),
        P(None, "mp"),
        P("mp"),
        P("mp", None),
        P(),
        P(None, "mp"),
        P("mp"),
        P("mp", None),
        P(),
        P(None, ("dp", "mp"), None),
        P(None, None, ("dp", "mp"), None),
        P("mp", "dp", None),
        P(None, "mp", "dp", None),
    )
    return jax.shard_map(
        per_device,
        mesh=mesh,
        in_specs=placed,
        out_specs=(
            P("dp", None),
            P("dp", None),
            P(None, ("dp", "mp")),
            P(None, ("dp", "mp"), None),
            P("mp", "dp", None),
            P(None, "mp"),
            P("mp", None),
            P(None, "mp"),
            P("mp", None),
            P(None, ("dp", "mp"), None),
            P("mp", "dp", None),
            P(None, None, ("dp", "mp"), None),
            P(None, "mp", "dp", None),
        ),
        check_vma=False,
    )
```
